512 devices in a mesh: pulse: 4 (over z_lo), range: 4 (over y), tile: 32 (over z_hi, x, core).
Axes of the slice: x: 4, y: 4, z: 16 (z_hi: 4, z_lo: 4; z = z_hi * 4 + z_lo), core: 2. Of those that a mesh axis runs over, the one named last changes fastest.
Arguments:
- echo: bfloat16 [2, 1024, 32768], P(None, ('pulse', 'tile'), 'range'), may hold values from -6 to 6
- replica: bfloat16 [2, 4096], replicated, may hold values from -0.09375 to 0.09375
- interp: bfloat16 [32, 256, 128], P('range'), may hold values from -0.375 to 0.375
- band_start: int32 [1024, 32, 4], P(('pulse', 'tile'), None, 'range'), may hold values from 0 to 7040, as said below
- visible: int32 [1024, 32], P(('pulse', 'tile')), may hold values 0 or 1
- doppler: int32 [1024], P(('pulse', 'tile')), may hold values from 0 to 8191
- range_step: int32 [1024], P(('pulse', 'tile')), may hold values from 0 to 4095
Outputs:
- image: float32 [2, 8192, 4096], P(None, ('tile', 'pulse'), 'range')
The draws below stay inside these ranges and needn't reach their ends.
Inputs may be any that keep to these rules, and one draw needn't show every extreme that they name: band_start is counted within the 8192 bins of range block b and is a multiple of 128; the values 0 and 7040 both occur.
All inputs are finite; a program needn't handle non-finite values. No bound on the sum of `visible` on one device may be relied on, other than what follows from the above.
Results may differ from the reference program's by a relative error of at most 0.0047.
Values may be sent and summed in bfloat16 or wider, within the bound.
No kernel may reach another device: no remote copies, remote signals or barrier semaphores. Data moves between devices by JAX's collectives and lax.ppermute only.
A program may use at most 64 MiB of HBM per device.

```python
import math
import jax
import jax.numpy as jnp
from jax import lax

CHIRP = 4096
SAMP_DEV = 8192
LINE_BLOCK = 128
RLINE_DEV = 1024
AZ_DEV = 64
TILES = 32
RBLOCKS = 4
NPULSE = 1024
NR = 32768
BAND = 1152
NA = 8192
NRG = 4096
N_PULSE = 4


def draw_band_start(key, part):
    largest_block = (SAMP_DEV - RLINE_DEV - LINE_BLOCK) // LINE_BLOCK
    values = jax.random.randint(key, (NPULSE, TILES, RBLOCKS), 0, largest_block + 1, dtype=jnp.int32) * LINE_BLOCK
    values = values.at[0, 0, 0].set(largest_block * LINE_BLOCK)
    return values.at[1, 0, 0].set(0)


def set_ends(result, key, least, high):
    place = [jax.random.randint(jax.random.fold_in(key, axis), (), 0, length) for axis, length in enumerate(result.shape)]
    main_axis = result.shape.index(max(result.shape))
    beside = place[:main_axis] + [(place[main_axis] + 1) % result.shape[main_axis]] + place[main_axis + 1:]
    return result.at[tuple(place)].set(least).at[tuple(beside)].set(high)


def level_of(rng, extent, shards, smallest, top_value):
    level = 1.0
    for dim, shards_of in shards:
        steps = jax.random.uniform(jax.random.fold_in(jax.random.fold_in(rng, 6), dim), (shards_of,), jnp.float32, smallest / len(shards), top_value / len(shards))
        level = level * jnp.repeat(jnp.exp(steps), extent[dim] // shards_of).reshape((-1,) + (1,) * (len(extent) - 1 - dim))
    return level


def scatter_about(stream_key, shape, deviation, limit, cuts=(), kind=jnp.bfloat16):
    array = deviation * jax.random.normal(stream_key, shape, jnp.float32)
    if cuts:
        array = array * level_of(stream_key, shape, cuts, -0.22, 0.18)
    return jnp.clip(array, -limit, limit).astype(kind)


def setup_inputs(seed: int = 0) -> dict:
    seeds = jax.random.split(jax.random.key(seed), 8)
    echo = scatter_about(seeds[0], (2, NPULSE, NR), 1.0, 6.0, ((1, 128), (2, 4)))
    replica = scatter_about(seeds[1], (2, CHIRP), CHIRP ** -0.5, 0.09375)
    interp = scatter_about(seeds[2], (NRG // LINE_BLOCK, 2 * LINE_BLOCK, LINE_BLOCK), (2 * LINE_BLOCK) ** -0.5, 0.375, ((0, 4),))
    band_start = draw_band_start(jax.random.fold_in(seeds[7], 71), 0)
    visible = set_ends((jax.random.randint(seeds[4], (NPULSE, TILES), 0, 4) < 3).astype(jnp.int32), jax.random.fold_in(seeds[4], 1), 0, 1)
    doppler = set_ends(jax.random.randint(seeds[5], (NPULSE,), 0, NA), jax.random.fold_in(seeds[5], 1), 0, NA - 1).astype(jnp.int32)
    range_step = set_ends(jax.random.randint(seeds[6], (NPULSE,), 0, NRG), jax.random.fold_in(seeds[6], 1), 0, NRG - 1).astype(jnp.int32)
    return {"echo": echo, "replica": replica, "interp": interp, "band_start": band_start, "visible": visible, "doppler": doppler, "range_step": range_step}


def toeplitz_block(padded, offset, block_width):
    segment = lax.dynamic_slice_in_dim(padded, offset, 2 * block_width + 1)
    repeated = jnp.tile(segment, block_width)[: 2 * block_width * block_width]
    skewed = repeated.reshape(block_width, 2 * block_width)
    return skewed[:, block_width:].T


def chirp_matrix(padded_real, padded_imag, offset, block_width):
    toep_real = toeplitz_block(padded_real, offset, block_width)
    toep_imag = toeplitz_block(padded_imag, offset, block_width)
    upper_rows = jnp.concatenate([toep_real, -toep_imag], axis=1)
    lower_rows = jnp.concatenate([toep_imag, toep_real], axis=1)
    return jnp.concatenate([upper_rows, lower_rows], axis=0)


def compress(extended, replica, block_width):
    chirp_len = replica.shape[1]
    pulses = extended.shape[1]
    total_blocks = extended.shape[2] // block_width
    out_blocks = total_blocks - chirp_len // block_width
    arranged = extended.reshape(2, pulses, total_blocks, block_width).transpose(1, 2, 0, 3)
    margin = jnp.zeros((2, block_width), replica.dtype)
    padded = jnp.concatenate([margin, replica, margin, margin[:, :1]], axis=1)

    def add_turn(turn_index, running):
        offset = (turn_index * block_width).astype(jnp.int32)
        matrix = chirp_matrix(padded[0], padded[1], offset, block_width)
        window = lax.dynamic_slice_in_dim(arranged, turn_index.astype(jnp.int32), out_blocks, 1)
        window = window.reshape(pulses * out_blocks, 2 * block_width)
        return running + jnp.dot(window, matrix, preferred_element_type=jnp.float32)

    start_total = jnp.zeros((pulses * out_blocks, 2 * block_width), jnp.float32)
    running = lax.fori_loop(0, chirp_len // block_width + 1, add_turn, start_total)
    shaped = running.reshape(pulses, out_blocks, 2, block_width).transpose(0, 2, 1, 3)
    return shaped.reshape(pulses, 2, out_blocks * block_width).astype(jnp.bfloat16)


def cut_bands(signals, first_bins, band_len):
    def cut_one(signal, first_bin):
        return lax.dynamic_slice_in_dim(signal, first_bin, band_len, 1)

    return jax.vmap(cut_one)(signals, first_bins)


def steer_lines(band_rows, interp_block, range_steps, first_line, range_total):
    pulses = band_rows.shape[0]
    block_count = interp_block.shape[0]
    line_block = interp_block.shape[2]
    pieces = band_rows.reshape(pulses, 2, block_count + 1, line_block)
    windows = jnp.concatenate([pieces[:, :, :-1], pieces[:, :, 1:]], axis=3)
    line_values = jnp.einsum("pcjb,jbl->pcjl", windows.astype(jnp.float32), interp_block.astype(jnp.float32))
    line_values = line_values.reshape(pulses, 2, block_count * line_block)
    line_number = first_line + jnp.arange(block_count * line_block, dtype=jnp.int32)
    phase_turns = (range_steps[:, None] * line_number[None, :]) % range_total
    phase_angle = phase_turns.astype(jnp.float32) * (2.0 * math.pi / range_total)
    cosine = jnp.cos(phase_angle)
    sine_part = jnp.sin(phase_angle)
    steered_real = line_values[:, 0] * cosine - line_values[:, 1] * sine_part
    steered_imag = line_values[:, 0] * sine_part + line_values[:, 1] * cosine
    return jnp.stack([steered_real, steered_imag], axis=1).astype(jnp.bfloat16)


def azimuth_factor(doppler_bins, visible_flags, line_number, azimuth_total, norm_scale):
    phase_turns = (line_number[:, None] * doppler_bins[None, :]) % azimuth_total
    phase_angle = phase_turns.astype(jnp.float32) * (2.0 * math.pi / azimuth_total)
    weight = visible_flags.astype(jnp.float32)[None, :] * norm_scale
    factor_real = (jnp.cos(phase_angle) * weight).astype(jnp.bfloat16)
    factor_imag = (jnp.sin(phase_angle) * weight).astype(jnp.bfloat16)
    return factor_real, factor_imag


def add_pulses(factor_real, factor_imag, steered):
    left_side = jnp.concatenate([factor_real, factor_imag], axis=1)
    steer_real = steered[:, 0]
    steer_imag = steered[:, 1]
    top_rows = jnp.concatenate([steer_real, steer_imag], axis=1)
    bottom_rows = jnp.concatenate([-steer_imag, steer_real], axis=1)
    right_side = jnp.concatenate([top_rows, bottom_rows], axis=0)
    return jnp.dot(left_side, right_side, preferred_element_type=jnp.float32)


def reference(echo, replica, interp, band_start, visible, doppler, range_step):
    half_chirp = CHIRP // 2
    block_width = min(256, half_chirp)
    extended = jnp.pad(echo, ((0, 0), (0, 0), (half_chirp, half_chirp)))
    compressed = compress(extended, replica, block_width)
    norm_scale = NPULSE ** -0.5
    range_pieces = RLINE_DEV // LINE_BLOCK
    strip_index = jnp.arange(N_PULSE * AZ_DEV, dtype=jnp.int32)

    def tile_image(tile_number):
        tile_flags = lax.dynamic_index_in_dim(visible, tile_number, 1, keepdims=False)
        line_number = tile_number * (N_PULSE * AZ_DEV) + strip_index
        factor_real, factor_imag = azimuth_factor(doppler, tile_flags, line_number, NA, norm_scale)
        columns = []
        for range_block in range(RBLOCKS):
            starts = lax.dynamic_index_in_dim(band_start[:, :, range_block], tile_number, 1, keepdims=False)
            band_rows = cut_bands(compressed, range_block * SAMP_DEV + starts, BAND)
            interp_block = interp[range_block * range_pieces:(range_block + 1) * range_pieces]
            steered = steer_lines(band_rows, interp_block, range_step, range_block * RLINE_DEV, NRG)
            summed = add_pulses(factor_real, factor_imag, steered)
            columns.append(summed.reshape(N_PULSE * AZ_DEV, 2, RLINE_DEV))
        return jnp.concatenate(columns, axis=2).transpose(1, 0, 2)

    tiles_out = lax.map(tile_image, jnp.arange(TILES, dtype=jnp.int32))
    return tiles_out.transpose(1, 0, 2, 3).reshape(2, NA, NRG)
```

```python
import math

import jax
import jax.numpy as jnp
from jax import lax
from jax.experimental import pallas as pl
from jax.experimental.pallas import tpu as pltpu
from jax.sharding import PartitionSpec as P

AZ_DEV = 64
LANES = 128
VMEM_LIMIT = 48 * 1024 * 1024


def skew_kernel(flip_ref, real_ref, imag_ref, minus_ref):
    count = real_ref.shape[1] // LANES
    for part, target in ((0, real_ref), (1, imag_ref)):
        for block in range(count):
            window = flip_ref[part : part + 1, block * LANES : (block + 2) * LANES]
            wide = jnp.broadcast_to(window, (LANES, 2 * LANES))
            rolled = pltpu.roll(wide, 1, 1, stride=1, stride_axis=0)[:, LANES:]
            place = slice(block * LANES, (block + 1) * LANES)
            target[:, place] = rolled.astype(jnp.bfloat16)
            if part == 1:
                minus_ref[:, place] = (-rolled).astype(jnp.bfloat16)


def skew_matrices(replica):
    taps = replica.shape[1]
    width = taps + LANES
    flipped = jnp.pad(jnp.flip(replica.astype(jnp.float32), 1), ((0, 0), (LANES, LANES)))
    shape = jax.ShapeDtypeStruct((LANES, width), jnp.bfloat16)
    return pl.pallas_call(
        skew_kernel,
        out_shape=(shape, shape, shape),
        name="skew_matrices",
        compiler_params=pltpu.CompilerParams(vmem_limit_bytes=VMEM_LIMIT),
        cost_estimate=pl.CostEstimate(flops=4000000, bytes_accessed=4 * 1024 * 1024, transcendentals=0),
    )(flipped)


def steer_kernel(
    left_ref, own_ref, right_ref, real_ref, imag_ref, minus_ref, interp_ref, target_ref,
    cos_ref, sin_ref, out_ref, even_ref, odd_ref, total_ref, band_ref,
):
    pulses = own_ref.shape[1]
    left_blocks = left_ref.shape[2] // LANES
    own_blocks = own_ref.shape[2] // LANES
    turns = real_ref.shape[1] // LANES
    blocks = 2 * left_blocks + own_blocks
    line_blocks = interp_ref.shape[0]
    rows = target_ref.shape[0]
    tiles = rows // pulses

    def cells(block):
        if block < left_blocks:
            ref, at = left_ref, block
        elif block < left_blocks + own_blocks:
            ref, at = own_ref, block - left_blocks
        else:
            ref, at = right_ref, block - left_blocks - own_blocks
        place = slice(at * LANES, (at + 1) * LANES)
        return jnp.concatenate(
            [ref[0, :, place].astype(jnp.float32), ref[1, :, place].astype(jnp.float32)], axis=1
        )

    for pair in range(blocks // 2):
        both = jnp.concatenate([cells(2 * pair), cells(2 * pair + 1)], axis=0)
        even_ref[pair] = both.astype(jnp.bfloat16)
        if 2 * pair + 2 < blocks:
            both = jnp.concatenate([cells(2 * pair + 1), cells(2 * pair + 2)], axis=0)
            odd_ref[pair] = both.astype(jnp.bfloat16)

    for turn in range(turns):
        source = even_ref if turn % 2 == 0 else odd_ref
        first = turn // 2
        window = source[first : first + own_blocks // 2].reshape(own_blocks * pulses, 2 * LANES)
        place = slice((turns - 1 - turn) * LANES, (turns - turn) * LANES)
        upper = jnp.concatenate([real_ref[:, place], minus_ref[:, place]], axis=1)
        lower = jnp.concatenate([imag_ref[:, place], real_ref[:, place]], axis=1)
        matrix = jnp.concatenate([upper, lower], axis=0)
        product = jnp.dot(window, matrix, preferred_element_type=jnp.float32)
        if turn == 0:
            total_ref[...] = product
        else:
            total_ref[...] += product

    compressed = total_ref[...].astype(jnp.bfloat16)
    column = lax.broadcasted_iota(jnp.int32, (rows, own_blocks * pulses), 1)
    for piece in range(line_blocks + 1):
        chooser = jnp.where(column == target_ref[...] + piece * pulses, 1.0, 0.0).astype(jnp.bfloat16)
        picked = jnp.dot(chooser, compressed, preferred_element_type=jnp.float32)
        band_ref[piece] = picked.astype(jnp.bfloat16)

    for line in range(line_blocks):
        values = []
        for part in range(2):
            half = slice(part * LANES, (part + 1) * LANES)
            pair = jnp.concatenate([band_ref[line, :, half], band_ref[line + 1, :, half]], axis=1)
            value = jnp.dot(pair, interp_ref[line], preferred_element_type=jnp.float32)
            values.append(value.reshape(tiles, pulses, LANES))
        place = slice(line * LANES, (line + 1) * LANES)
        cosine = cos_ref[:, place][None]
        sine = sin_ref[:, place][None]
        steer_real = values[0] * cosine - values[1] * sine
        steer_imag = values[0] * sine + values[1] * cosine
        steered = jnp.concatenate([steer_real, steer_imag], axis=1)
        out_ref[:, :, place] = steered.astype(jnp.bfloat16)


def steered_values(left, echo, right, skewed, interp, targets, cosine, sine):
    pulses = echo.shape[1]
    own_blocks = echo.shape[2] // LANES
    blocks = own_blocks + 2 * (left.shape[2] // LANES)
    rows = targets.shape[0]
    line_blocks = interp.shape[0]
    return pl.pallas_call(
        steer_kernel,
        out_shape=jax.ShapeDtypeStruct((rows // pulses, 2 * pulses, line_blocks * LANES), jnp.bfloat16),
        scratch_shapes=[
            pltpu.VMEM((blocks // 2, 2 * pulses, 2 * LANES), jnp.bfloat16),
            pltpu.VMEM((blocks // 2, 2 * pulses, 2 * LANES), jnp.bfloat16),
            pltpu.VMEM((own_blocks * pulses, 2 * LANES), jnp.float32),
            pltpu.VMEM((line_blocks + 1, rows, 2 * LANES), jnp.bfloat16),
        ],
        name="steered_values",
        compiler_params=pltpu.CompilerParams(vmem_limit_bytes=VMEM_LIMIT),
        cost_estimate=pl.CostEstimate(flops=4000000000, bytes_accessed=6 * 1024 * 1024, transcendentals=0),
    )(left, echo, right, *skewed, interp, targets, cosine, sine)


def local(echo, replica, interp, band_start, visible, doppler, range_step):
    half_chirp = replica.shape[1] // 2
    pulses_dev = echo.shape[1]
    line_block = interp.shape[2]
    lines_dev = interp.shape[0] * line_block
    tile_count = lax.axis_size("tile")
    pulse_count = lax.axis_size("pulse")
    range_count = lax.axis_size("range")
    range_total = lines_dev * range_count
    azimuth_total = AZ_DEV * pulse_count * tile_count
    norm_scale = (pulses_dev * pulse_count * tile_count) ** (-0.5)
    tile_number = lax.axis_index("tile")
    first_line = lax.axis_index("range") * lines_dev

    up = [(i, i + 1) for i in range(range_count - 1)]
    down = [(i + 1, i) for i in range(range_count - 1)]
    left = lax.ppermute(echo[:, :, -half_chirp:], "range", up)
    right = lax.ppermute(echo[:, :, :half_chirp], "range", down)
    skewed = skew_matrices(replica)

    doppler_rows = lax.optimization_barrier(jnp.broadcast_to(doppler[:, None], (pulses_dev, LANES)))
    doppler_rows = lax.all_gather(doppler_rows, "tile", axis=0, tiled=True)
    doppler_rows = lax.optimization_barrier(doppler_rows)
    doppler_in = doppler_rows[:, 0].reshape(tile_count, 1, pulses_dev)

    line_number = first_line + jnp.arange(lines_dev, dtype=jnp.int32)
    phase_turns = range_step[:, None] * line_number[None, :] % range_total
    phase_angle = phase_turns.astype(jnp.float32) * (2.0 * math.pi / range_total)
    cosine = jnp.cos(phase_angle)
    sine = jnp.sin(phase_angle)

    pulse_index = jnp.arange(pulses_dev, dtype=jnp.int32)[:, None]
    targets = band_start[:, :, 0] // LANES * pulses_dev + pulse_index
    targets = jnp.where(visible != 0, targets, -(1 << 20)).T.reshape(tile_count * pulses_dev, 1)

    steered = steered_values(left, echo, right, skewed, interp, targets, cosine, sine)
    arrived = lax.all_to_all(steered, "tile", 0, 0, tiled=True)
    columns = tile_count * 2 * pulses_dev
    arrived = arrived.reshape(columns, lines_dev)

    quarter = azimuth_total // 4
    shape = (pulse_count, 2, AZ_DEV, tile_count, 2, pulses_dev)
    axes = [lax.broadcasted_iota(jnp.int32, shape[:3], axis) for axis in range(3)]
    lines = tile_number * (pulse_count * AZ_DEV) + axes[0] * AZ_DEV + axes[2]
    lines = lines.reshape(-1, 1)
    out_part = axes[1].reshape(-1, 1)
    in_part = jnp.broadcast_to(
        jnp.arange(2, dtype=jnp.int32)[None, :, None], (tile_count, 2, pulses_dev)
    ).reshape(1, -1)
    bins = jnp.broadcast_to(doppler_in, (tile_count, 2, pulses_dev)).reshape(1, -1)
    azimuth_turns = (lines * bins + (in_part - out_part) * quarter) % azimuth_total
    azimuth_angle = azimuth_turns.astype(jnp.float32) * (2.0 * math.pi / azimuth_total)
    factor = (jnp.cos(azimuth_angle) * norm_scale).astype(jnp.bfloat16)
    factor = lax.optimization_barrier(factor)

    partial_image = jnp.dot(factor, arrived, preferred_element_type=jnp.float32).astype(jnp.bfloat16)
    image_rows = lax.psum_scatter(partial_image, "pulse", scatter_dimension=0, tiled=True)
    return image_rows.astype(jnp.float32).reshape(2, AZ_DEV, lines_dev)


def solution(mesh):
    in_specs = (
        P(None, ("pulse", "tile"), "range"),
        P(),
        P("range", None, None),
        P(("pulse", "tile"), None, "range"),
        P(("pulse", "tile"), None),
        P(("pulse", "tile")),
        P(("pulse", "tile")),
    )
    out_specs = P(None, ("tile", "pulse"), "range")
    return jax.shard_map(local, mesh=mesh, in_specs=in_specs, out_specs=out_specs, check_vma=False)
```

```python
import functools
import math

import jax
import jax.numpy as jnp
from jax import lax
from jax.experimental import pallas as pl
from jax.experimental.pallas import tpu as pltpu
from jax.sharding import PartitionSpec as P

AZ_DEV = 64
LANES = 128
SUB = 8
GROUP = 8
DIGIT = 128
HIDDEN = 128
NOTE_STEP = 32
NOTE_BIN = 34
VMEM_LIMIT = 14 * 1024 * 1024

SINE = tuple((-1.0) ** n * (2.0 * math.pi) ** (2 * n + 1) / math.factorial(2 * n + 1) for n in range(8))


def cosine_of_turns(turns, total):
    away = jnp.abs(turns.astype(jnp.float32) * (1.0 / total) - 0.5) - 0.25
    square = away * away
    value = jnp.full_like(away, SINE[-1])
    for factor in SINE[-2::-1]:
        value = value * square + factor
    return value * away


def params(**extra):
    return pltpu.CompilerParams(vmem_limit_bytes=VMEM_LIMIT, **extra)


def pair_rows(first, second):
    return jnp.concatenate([first, second], axis=0).astype(jnp.bfloat16)


def block_cells(ref, block):
    place = slice(block * LANES, (block + 1) * LANES)
    return jnp.concatenate(
        [ref[0, :, place].astype(jnp.float32), ref[1, :, place].astype(jnp.float32)], axis=1
    )


def arrange(ref, even_ref, odd_ref):
    blocks = ref.shape[2] // LANES
    nothing = jnp.zeros((SUB, 2 * LANES), jnp.float32)
    for pair in range(blocks // 2):
        first = block_cells(ref, 2 * pair)
        second = block_cells(ref, 2 * pair + 1)
        third = block_cells(ref, 2 * pair + 2) if 2 * pair + 2 < blocks else nothing
        even_ref[pair] = pair_rows(first, second)
        odd_ref[pair] = pair_rows(second, third)


def rows_from(even_ref, odd_ref, first, count):
    source = even_ref if first % 2 == 0 else odd_ref
    pairs = (count + 1) // 2
    start = first // 2
    return source[start : start + pairs].reshape(pairs * 2 * SUB, 2 * LANES)


def turn_matrix(real_ref, imag_ref, minus_ref, turn):
    turns = real_ref.shape[1] // LANES
    place = slice((turns - 1 - turn) * LANES, (turns - turn) * LANES)
    upper = jnp.concatenate([real_ref[:, place], minus_ref[:, place]], axis=1)
    lower = jnp.concatenate([imag_ref[:, place], real_ref[:, place]], axis=1)
    return jnp.concatenate([upper, lower], axis=0)


def own_kernel(replica_ref, own_ref, real_ref, imag_ref, minus_ref, total_ref, flip_ref, even_ref, odd_ref):
    taps = replica_ref.shape[1] // LANES
    own_blocks = own_ref.shape[2] // LANES
    half = taps // 2
    row = lax.broadcasted_iota(jnp.int32, (LANES, LANES), 0)
    column = lax.broadcasted_iota(jnp.int32, (LANES, LANES), 1)
    mirror = jnp.where(row + column == LANES - 1, 1.0, 0.0).astype(jnp.bfloat16)
    pieces = [
        replica_ref[part : part + 1, block * LANES : (block + 1) * LANES].astype(jnp.float32)
        for part in range(2)
        for block in range(taps)
    ]
    stacked = jnp.concatenate(pieces, axis=0).astype(jnp.bfloat16)
    flip_ref[...] = jnp.dot(stacked, mirror, preferred_element_type=jnp.float32)
    nothing = jnp.zeros((1, LANES), jnp.float32)
    for part, target in ((0, real_ref), (1, imag_ref)):
        base = part * taps
        for block in range(taps + 1):
            before = flip_ref[base + taps - block : base + taps - block + 1] if block else nothing
            after = flip_ref[base + taps - 1 - block : base + taps - block] if block < taps else nothing
            wide = jnp.broadcast_to(jnp.concatenate([before, after], axis=1), (LANES, 2 * LANES))
            rolled = pltpu.roll(wide, 1, 1, stride=1, stride_axis=0)[:, LANES:]
            place = slice(block * LANES, (block + 1) * LANES)
            target[:, place] = rolled.astype(jnp.bfloat16)
            if part == 1:
                minus_ref[:, place] = (-rolled).astype(jnp.bfloat16)

    arrange(own_ref, even_ref, odd_ref)
    for turn in [half] + [t for t in range(taps + 1) if t != half]:
        matrix = turn_matrix(real_ref, imag_ref, minus_ref, turn)
        first_in = max(0, turn - half)
        first_out = max(0, half - turn)
        count = own_blocks - abs(turn - half)
        window = rows_from(even_ref, odd_ref, first_in, count)
        product = jnp.dot(window, matrix, preferred_element_type=jnp.float32)
        place = slice(first_out * SUB, (first_out + count) * SUB)
        if turn == half:
            total_ref[...] = product
        else:
            total_ref[place] += product[: count * SUB]


def own_part(replica, echo):
    taps = replica.shape[1]
    blocks = echo.shape[2] // LANES
    skewed = jax.ShapeDtypeStruct((LANES, taps + LANES), jnp.bfloat16)
    cells = pltpu.VMEM((blocks // 2, 2 * SUB, 2 * LANES), jnp.bfloat16)
    return pl.pallas_call(
        own_kernel,
        out_shape=(skewed, skewed, skewed, jax.ShapeDtypeStruct((blocks * SUB, 2 * LANES), jnp.float32)),
        scratch_shapes=[pltpu.VMEM((2 * taps // LANES, LANES), jnp.float32), cells, cells],
        name="own_part",
        compiler_params=params(),
        cost_estimate=pl.CostEstimate(flops=2000000000, bytes_accessed=8 * 1024 * 1024, transcendentals=0),
    )(replica, echo)


def edge_kernel(
    step_ref, bin_ref, left_ref, right_ref, real_ref, imag_ref, minus_ref, total_ref, band_ref, visible_ref,
    out_ref, sum_ref, even_ref, odd_ref, even2_ref, odd2_ref, note_ref,
):
    rows = total_ref.shape[0]
    own_blocks = rows // SUB
    half = left_ref.shape[2] // LANES
    arrange(left_ref, even_ref, odd_ref)
    arrange(right_ref, even2_ref, odd2_ref)
    sum_ref[...] = total_ref[...]
    for turn in range(half):
        matrix = turn_matrix(real_ref, imag_ref, minus_ref, turn)
        count = half - turn
        window = rows_from(even_ref, odd_ref, turn, count)
        product = jnp.dot(window, matrix, preferred_element_type=jnp.float32)
        sum_ref[: count * SUB] += product[: count * SUB]
    for turn in range(half + 1, 2 * half + 1):
        matrix = turn_matrix(real_ref, imag_ref, minus_ref, turn)
        count = turn - half
        window = rows_from(even2_ref, odd2_ref, 0, count)
        product = jnp.dot(window, matrix, preferred_element_type=jnp.float32)
        sum_ref[(own_blocks - count) * SUB :] += product[: count * SUB]
    out_ref[:rows] = sum_ref[...].astype(jnp.bfloat16)
    pulse = lax.broadcasted_iota(jnp.int32, (SUB, LANES), 0)
    lane = lax.broadcasted_iota(jnp.int32, (SUB, LANES), 1)
    note = jnp.zeros((SUB, LANES), jnp.int32)
    for index in range(SUB):
        step = step_ref[index]
        bin_here = bin_ref[index]
        for at, digit in enumerate((step // DIGIT, step % DIGIT, bin_here // DIGIT, bin_here % DIGIT)):
            note = jnp.where((pulse == index) & (lane == NOTE_STEP + at), digit, note)
    note_ref[...] = note.astype(jnp.float32)
    bands = jnp.where(visible_ref[...] != 0, band_ref[...] // LANES, HIDDEN)
    note_ref[:, : bands.shape[1]] = bands.astype(jnp.float32)
    nothing = jnp.zeros((SUB, LANES), jnp.float32)
    out_ref[rows:, :LANES] = pair_rows(note_ref[...], nothing)
    out_ref[rows:, LANES:] = pair_rows(nothing, nothing)


def edge_part(left, right, skewed, total, bands, visible, steps, bins):
    half = left.shape[2] // LANES
    cells = pltpu.VMEM((half // 2, 2 * SUB, 2 * LANES), jnp.bfloat16)
    rows = total.shape[0]
    return pl.pallas_call(
        edge_kernel,
        out_shape=jax.ShapeDtypeStruct((rows + 2 * SUB, 2 * LANES), jnp.bfloat16),
        in_specs=[pl.BlockSpec(memory_space=pltpu.SMEM)] * 2 + [pl.BlockSpec(memory_space=pltpu.VMEM)] * 8,
        scratch_shapes=[pltpu.VMEM(total.shape, jnp.float32), cells, cells, cells, cells]
        + [pltpu.VMEM((SUB, LANES), jnp.float32)],
        name="edge_part",
        compiler_params=params(),
        cost_estimate=pl.CostEstimate(flops=300000000, bytes_accessed=4 * 1024 * 1024, transcendentals=0),
    )(steps, bins, left, right, *skewed, total, bands, visible)


def steer_kernel(lines_total, hops, *refs):
    chunk_refs, (interp_ref, out_ref, band_ref) = refs[:-3], refs[-3:]
    line_blocks = interp_ref.shape[0]
    lines = line_blocks * LANES
    far = lax.axis_size("tile") // GROUP
    group = lax.rem(lax.axis_index("tile") // GROUP + hops, far)
    first_line = lax.axis_index("range") * lines
    note_rows = 2 * SUB
    rows = GROUP * SUB
    for chunk, parts in enumerate(chunk_refs):
        whole = parts[...]
        count = whole.shape[0] - note_rows
        compressed = whole[:count]
        note = whole[count:].astype(jnp.float32)[:SUB, :LANES]
        lane = lax.broadcasted_iota(jnp.int32, (SUB, LANES), 1)

        def pick(index):
            return jnp.sum(jnp.where(lane == index, note, 0.0), axis=1, keepdims=True).astype(jnp.int32)

        pulse = lax.broadcasted_iota(jnp.int32, (SUB, 1), 0)
        wanted = jnp.concatenate([pick(group * GROUP + tile) * SUB + pulse for tile in range(GROUP)], axis=0)
        column = lax.broadcasted_iota(jnp.int32, (rows, count), 1)
        away = column - wanted
        for piece in range(line_blocks + 1):
            chooser = jnp.where(away == piece * SUB, 1.0, 0.0).astype(jnp.bfloat16)
            picked = jnp.dot(chooser, compressed, preferred_element_type=jnp.float32)
            band_ref[piece] = picked.astype(jnp.bfloat16)

        step = pick(NOTE_STEP) * DIGIT + pick(NOTE_STEP + 1)
        number = first_line + lax.broadcasted_iota(jnp.int32, (SUB, lines), 1)
        turns = (step * number) & (lines_total - 1)
        cosine = cosine_of_turns(turns, lines_total)
        sine = cosine_of_turns((turns - lines_total // 4) & (lines_total - 1), lines_total)

        for line in range(line_blocks):
            both = []
            for part in range(2):
                half = slice(part * LANES, (part + 1) * LANES)
                both.append(jnp.concatenate([band_ref[line, :, half], band_ref[line + 1, :, half]], axis=1))
            values = jnp.dot(
                jnp.concatenate(both, axis=0), interp_ref[line], preferred_element_type=jnp.float32
            )
            real = values[:rows].reshape(GROUP, SUB, LANES)
            imag = values[rows:].reshape(GROUP, SUB, LANES)
            at = slice(line * LANES, (line + 1) * LANES)
            cos_here = cosine[:, at][None]
            sin_here = sine[:, at][None]
            steered = jnp.concatenate(
                [real * cos_here - imag * sin_here, real * sin_here + imag * cos_here], axis=1
            )
            out_ref[:, chunk * 2 * SUB : (chunk + 1) * 2 * SUB, at] = steered.astype(jnp.bfloat16)
        tail = jnp.concatenate([note, note], axis=0).astype(jnp.bfloat16)
        out_ref[:, chunk * 2 * SUB : (chunk + 1) * 2 * SUB, lines:] = jnp.broadcast_to(
            tail[None], (GROUP, 2 * SUB, LANES)
        )


def steer_part(chunks, interp, lines_total, hops):
    line_blocks = interp.shape[0]
    lines = line_blocks * LANES
    return pl.pallas_call(
        functools.partial(steer_kernel, lines_total, hops),
        out_shape=jax.ShapeDtypeStruct((GROUP, len(chunks) * 2 * SUB, lines + LANES), jnp.bfloat16),
        scratch_shapes=[pltpu.VMEM((line_blocks + 1, GROUP * SUB, 2 * LANES), jnp.bfloat16)],
        name="steer_part",
        compiler_params=params(),
        cost_estimate=pl.CostEstimate(
            flops=20000000000 * len(chunks), bytes_accessed=1024, transcendentals=0
        ),
    )(*chunks, interp)


def image_kernel(total, scale, first, last, values_ref, *refs):
    rows = values_ref.shape[0] * values_ref.shape[1]
    lines = values_ref.shape[2] - LANES
    note = values_ref[:, :, lines:].reshape(rows, LANES).astype(jnp.float32)
    turned = note.T
    bins = turned[NOTE_BIN : NOTE_BIN + 1] * DIGIT + turned[NOTE_BIN + 1 : NOTE_BIN + 2]
    bins = bins.astype(jnp.int32)
    in_part = (lax.broadcasted_iota(jnp.int32, (1, rows), 1) // SUB) & 1
    groups = lax.axis_size("pulse")
    first_line = lax.axis_index("tile") * (groups * AZ_DEV)
    me = lax.axis_index("pulse")
    block = 2 * AZ_DEV
    index = lax.broadcasted_iota(jnp.int32, (block, 1), 0)
    out_part = index // AZ_DEV
    values = values_ref[:, :, :lines].reshape(rows, lines)
    if first:
        outs = refs
    else:
        before_ref, outs = refs[0], refs[1:]
    for hop in range(groups):
        owner = lax.rem(me + hop, groups)
        line = first_line + owner * AZ_DEV + index % AZ_DEV
        turns = (line * bins + (in_part - out_part) * (total // 4)) & (total - 1)
        factor = (cosine_of_turns(turns, total) * scale).astype(jnp.bfloat16)
        image = jnp.dot(factor, values, preferred_element_type=jnp.float32)
        if not first:
            image = image + before_ref[hop]
        if not last:
            outs[0][hop] = image
        elif hop == 0:
            outs[0][...] = image
        else:
            outs[hop][...] = image.astype(jnp.bfloat16)


def image_part(values, before, last, total, scale):
    groups = lax.axis_size("pulse")
    lines = values.shape[2] - LANES
    block = 2 * AZ_DEV
    if last:
        out_shape = (jax.ShapeDtypeStruct((block, lines), jnp.float32),) + tuple(
            jax.ShapeDtypeStruct((block, lines), jnp.bfloat16) for _ in range(groups - 1)
        )
    else:
        out_shape = jax.ShapeDtypeStruct((groups, block, lines), jnp.float32)
    operands = (values,) + (() if before is None else (before,))
    return pl.pallas_call(
        functools.partial(image_kernel, total, scale, before is None, last),
        out_shape=out_shape,
        name="image_part",
        compiler_params=params(),
        cost_estimate=pl.CostEstimate(flops=20000000000, bytes_accessed=1024, transcendentals=0),
    )(*operands)


def local(echo, replica, interp, band_start, visible, doppler, range_step):
    half_chirp = replica.shape[1] // 2
    pulses_dev = echo.shape[1]
    lines_dev = interp.shape[0] * interp.shape[2]
    tile_count = lax.axis_size("tile")
    pulse_count = lax.axis_size("pulse")
    range_count = lax.axis_size("range")
    range_total = lines_dev * range_count
    azimuth_total = AZ_DEV * pulse_count * tile_count
    norm_scale = (pulses_dev * pulse_count * tile_count) ** (-0.5)
    far = tile_count // GROUP

    up = [(i, i + 1) for i in range(range_count - 1)]
    down = [(i + 1, i) for i in range(range_count - 1)]
    left = lax.ppermute(echo[:, :, -half_chirp:], "range", up)
    right = lax.ppermute(echo[:, :, :half_chirp], "range", down)
    *skewed, total = own_part(replica, echo)

    bands = band_start.reshape(pulses_dev, tile_count)
    mine = edge_part(left, right, skewed, total, bands, visible, range_step, doppler)

    def group_shift(hops):
        return [
            (h * GROUP + i, (h + hops) % far * GROUP + i) for h in range(far) for i in range(GROUP)
        ]

    groups = [[h * GROUP + i for i in range(GROUP)] for h in range(far)]

    def steer(chunks, hops=0):
        return steer_part(chunks, interp, range_total, hops)

    def exchange(steered):
        return lax.all_to_all(steered, "tile", 0, 0, axis_index_groups=groups, tiled=True)

    def add_image(values, before, last=False):
        return image_part(values, before, last, azimuth_total, norm_scale)

    below = lax.ppermute(mine, "tile", group_shift(1))
    above = lax.ppermute(mine, "tile", group_shift(-1))
    steered = steer([mine], far // 2)
    opposite = lax.ppermute(exchange(steered), "tile", group_shift(far // 2))
    mine, _ = lax.optimization_barrier((mine, steered))
    image = add_image(exchange(steer([mine])), None)
    image = add_image(exchange(steer([below, above])), image)
    image = add_image(opposite, image, last=True)

    kept, *sent = image
    for hop, cells in enumerate(sent, 1):
        pairs = [(i, (i + hop) % pulse_count) for i in range(pulse_count)]
        kept = kept + lax.ppermute(cells, "pulse", pairs).astype(jnp.float32)
    return kept.reshape(2, AZ_DEV, lines_dev)


def solution(mesh):
    in_specs = (
        P(None, ("pulse", "tile"), "range"),
        P(),
        P("range", None, None),
        P(("pulse", "tile"), None, "range"),
        P(("pulse", "tile"), None),
        P(("pulse", "tile")),
        P(("pulse", "tile")),
    )
    out_specs = P(None, ("tile", "pulse"), "range")
    return jax.shard_map(local, mesh=mesh, in_specs=in_specs, out_specs=out_specs, check_vma=False)
```

```python
import functools
import math

import jax
import jax.numpy as jnp
from jax import lax
from jax.experimental import pallas as pl
from jax.experimental.pallas import tpu as pltpu
from jax.sharding import PartitionSpec as P

AZ_DEV = 64
LANES = 128
SUB = 8
GROUP = 8
DIGIT = 128
HIDDEN = 128
NOTE_STEP = 32
NOTE_BIN = 34
VMEM_LIMIT = 14 * 1024 * 1024
IMAGE_COST = 20000000000
STEER_COST = 20000000000

SINE = tuple((-1.0) ** n * (2.0 * math.pi) ** (2 * n + 1) / math.factorial(2 * n + 1) for n in range(8))


def cosine_of_turns(turns, total):
    away = jnp.abs(turns.astype(jnp.float32) * (1.0 / total) - 0.5) - 0.25
    square = away * away
    value = jnp.full_like(away, SINE[-1])
    for factor in SINE[-2::-1]:
        value = value * square + factor
    return value * away


def params(**extra):
    return pltpu.CompilerParams(vmem_limit_bytes=VMEM_LIMIT, **extra)


def pair_rows(first, second):
    return jnp.concatenate([first, second], axis=0).astype(jnp.bfloat16)


def block_cells(ref, block):
    place = slice(block * LANES, (block + 1) * LANES)
    return jnp.concatenate(
        [ref[0, :, place].astype(jnp.float32), ref[1, :, place].astype(jnp.float32)], axis=1
    )


def arrange(ref, even_ref, odd_ref):
    blocks = ref.shape[2] // LANES
    nothing = jnp.zeros((SUB, 2 * LANES), jnp.float32)
    for pair in range(blocks // 2):
        first = block_cells(ref, 2 * pair)
        second = block_cells(ref, 2 * pair + 1)
        third = block_cells(ref, 2 * pair + 2) if 2 * pair + 2 < blocks else nothing
        even_ref[pair] = pair_rows(first, second)
        odd_ref[pair] = pair_rows(second, third)


def rows_from(even_ref, odd_ref, first, count):
    source = even_ref if first % 2 == 0 else odd_ref
    pairs = (count + 1) // 2
    start = first // 2
    return source[start : start + pairs].reshape(pairs * 2 * SUB, 2 * LANES)


def turn_matrix(real_ref, imag_ref, minus_ref, turn):
    turns = real_ref.shape[1] // LANES
    place = slice((turns - 1 - turn) * LANES, (turns - turn) * LANES)
    upper = jnp.concatenate([real_ref[:, place], minus_ref[:, place]], axis=1)
    lower = jnp.concatenate([imag_ref[:, place], real_ref[:, place]], axis=1)
    return jnp.concatenate([upper, lower], axis=0)


def own_kernel(replica_ref, own_ref, real_ref, imag_ref, minus_ref, total_ref, flip_ref, even_ref, odd_ref):
    taps = replica_ref.shape[1] // LANES
    own_blocks = own_ref.shape[2] // LANES
    half = taps // 2
    row = lax.broadcasted_iota(jnp.int32, (LANES, LANES), 0)
    column = lax.broadcasted_iota(jnp.int32, (LANES, LANES), 1)
    mirror = jnp.where(row + column == LANES - 1, 1.0, 0.0).astype(jnp.bfloat16)
    pieces = [
        replica_ref[part : part + 1, block * LANES : (block + 1) * LANES].astype(jnp.float32)
        for part in range(2)
        for block in range(taps)
    ]
    stacked = jnp.concatenate(pieces, axis=0).astype(jnp.bfloat16)
    flip_ref[...] = jnp.dot(stacked, mirror, preferred_element_type=jnp.float32)
    nothing = jnp.zeros((1, LANES), jnp.float32)
    for part, target in ((0, real_ref), (1, imag_ref)):
        base = part * taps
        for block in range(taps + 1):
            before = flip_ref[base + taps - block : base + taps - block + 1] if block else nothing
            after = flip_ref[base + taps - 1 - block : base + taps - block] if block < taps else nothing
            wide = jnp.broadcast_to(jnp.concatenate([before, after], axis=1), (LANES, 2 * LANES))
            rolled = pltpu.roll(wide, 1, 1, stride=1, stride_axis=0)[:, LANES:]
            place = slice(block * LANES, (block + 1) * LANES)
            target[:, place] = rolled.astype(jnp.bfloat16)
            if part == 1:
                minus_ref[:, place] = (-rolled).astype(jnp.bfloat16)

    arrange(own_ref, even_ref, odd_ref)
    for turn in [half] + [t for t in range(taps + 1) if t != half]:
        matrix = turn_matrix(real_ref, imag_ref, minus_ref, turn)
        first_in = max(0, turn - half)
        first_out = max(0, half - turn)
        count = own_blocks - abs(turn - half)
        window = rows_from(even_ref, odd_ref, first_in, count)
        product = jnp.dot(window, matrix, preferred_element_type=jnp.float32)
        place = slice(first_out * SUB, (first_out + count) * SUB)
        if turn == half:
            total_ref[...] = product
        else:
            total_ref[place] += product[: count * SUB]


def own_part(replica, echo):
    taps = replica.shape[1]
    blocks = echo.shape[2] // LANES
    skewed = jax.ShapeDtypeStruct((LANES, taps + LANES), jnp.bfloat16)
    cells = pltpu.VMEM((blocks // 2, 2 * SUB, 2 * LANES), jnp.bfloat16)
    return pl.pallas_call(
        own_kernel,
        out_shape=(skewed, skewed, skewed, jax.ShapeDtypeStruct((blocks * SUB, 2 * LANES), jnp.float32)),
        scratch_shapes=[pltpu.VMEM((2 * taps // LANES, LANES), jnp.float32), cells, cells],
        name="own_part",
        compiler_params=params(),
        cost_estimate=pl.CostEstimate(flops=2000000000, bytes_accessed=8 * 1024 * 1024, transcendentals=0),
    )(replica, echo)


def edge_kernel(
    step_ref, bin_ref, left_ref, right_ref, real_ref, imag_ref, minus_ref, total_ref, band_ref, visible_ref,
    out_ref, sum_ref, even_ref, odd_ref, even2_ref, odd2_ref, note_ref,
):
    rows = total_ref.shape[0]
    own_blocks = rows // SUB
    half = left_ref.shape[2] // LANES
    arrange(left_ref, even_ref, odd_ref)
    arrange(right_ref, even2_ref, odd2_ref)
    sum_ref[...] = total_ref[...]
    for turn in range(half):
        matrix = turn_matrix(real_ref, imag_ref, minus_ref, turn)
        count = half - turn
        window = rows_from(even_ref, odd_ref, turn, count)
        product = jnp.dot(window, matrix, preferred_element_type=jnp.float32)
        sum_ref[: count * SUB] += product[: count * SUB]
    for turn in range(half + 1, 2 * half + 1):
        matrix = turn_matrix(real_ref, imag_ref, minus_ref, turn)
        count = turn - half
        window = rows_from(even2_ref, odd2_ref, 0, count)
        product = jnp.dot(window, matrix, preferred_element_type=jnp.float32)
        sum_ref[(own_blocks - count) * SUB :] += product[: count * SUB]
    out_ref[:rows] = sum_ref[...].astype(jnp.bfloat16)
    pulse = lax.broadcasted_iota(jnp.int32, (SUB, LANES), 0)
    lane = lax.broadcasted_iota(jnp.int32, (SUB, LANES), 1)
    note = jnp.zeros((SUB, LANES), jnp.int32)
    for index in range(SUB):
        step = step_ref[index]
        bin_here = bin_ref[index]
        for at, digit in enumerate((step // DIGIT, step % DIGIT, bin_here // DIGIT, bin_here % DIGIT)):
            note = jnp.where((pulse == index) & (lane == NOTE_STEP + at), digit, note)
    note_ref[...] = note.astype(jnp.float32)
    bands = jnp.where(visible_ref[...] != 0, band_ref[...] // LANES, HIDDEN)
    note_ref[:, : bands.shape[1]] = bands.astype(jnp.float32)
    nothing = jnp.zeros((SUB, LANES), jnp.float32)
    out_ref[rows:, :LANES] = pair_rows(note_ref[...], nothing)
    out_ref[rows:, LANES:] = pair_rows(nothing, nothing)


def edge_part(left, right, skewed, total, bands, visible, steps, bins):
    half = left.shape[2] // LANES
    cells = pltpu.VMEM((half // 2, 2 * SUB, 2 * LANES), jnp.bfloat16)
    rows = total.shape[0]
    return pl.pallas_call(
        edge_kernel,
        out_shape=jax.ShapeDtypeStruct((rows + 2 * SUB, 2 * LANES), jnp.bfloat16),
        in_specs=[pl.BlockSpec(memory_space=pltpu.SMEM)] * 2 + [pl.BlockSpec(memory_space=pltpu.VMEM)] * 8,
        scratch_shapes=[pltpu.VMEM(total.shape, jnp.float32), cells, cells, cells, cells]
        + [pltpu.VMEM((SUB, LANES), jnp.float32)],
        name="edge_part",
        compiler_params=params(),
        cost_estimate=pl.CostEstimate(flops=300000000, bytes_accessed=4 * 1024 * 1024, transcendentals=0),
    )(steps, bins, left, right, *skewed, total, bands, visible)


def steer_kernel(lines_total, group_hops, *refs):
    chunk_refs, (interp_ref, out_ref, band_ref) = refs[:-3], refs[-3:]
    line_blocks = interp_ref.shape[0]
    lines = line_blocks * LANES
    far = lax.axis_size("tile") // GROUP
    first_line = lax.axis_index("range") * lines
    note_rows = 2 * SUB
    rows = GROUP * SUB
    for chunk, parts in enumerate(chunk_refs):
        whole = parts[...]
        count = whole.shape[0] - note_rows
        compressed = whole[:count]
        group = lax.rem(lax.axis_index("tile") // GROUP + group_hops[chunk], far)
        note = whole[count:].astype(jnp.float32)[:SUB, :LANES]
        lane = lax.broadcasted_iota(jnp.int32, (SUB, LANES), 1)

        def pick(index):
            return jnp.sum(jnp.where(lane == index, note, 0.0), axis=1, keepdims=True).astype(jnp.int32)

        pulse = lax.broadcasted_iota(jnp.int32, (SUB, 1), 0)
        wanted = jnp.concatenate([pick(group * GROUP + tile) * SUB + pulse for tile in range(GROUP)], axis=0)
        column = lax.broadcasted_iota(jnp.int32, (rows, count), 1)
        away = column - wanted
        for piece in range(line_blocks + 1):
            chooser = jnp.where(away == piece * SUB, 1.0, 0.0).astype(jnp.bfloat16)
            picked = jnp.dot(chooser, compressed, preferred_element_type=jnp.float32)
            band_ref[piece] = picked.astype(jnp.bfloat16)

        step = pick(NOTE_STEP) * DIGIT + pick(NOTE_STEP + 1)
        number = first_line + lax.broadcasted_iota(jnp.int32, (SUB, lines), 1)
        turns = (step * number) & (lines_total - 1)
        cosine = cosine_of_turns(turns, lines_total)
        sine = cosine_of_turns((turns - lines_total // 4) & (lines_total - 1), lines_total)

        for line in range(line_blocks):
            both = []
            for part in range(2):
                half = slice(part * LANES, (part + 1) * LANES)
                both.append(jnp.concatenate([band_ref[line, :, half], band_ref[line + 1, :, half]], axis=1))
            values = jnp.dot(
                jnp.concatenate(both, axis=0), interp_ref[line], preferred_element_type=jnp.float32
            )
            real = values[:rows].reshape(GROUP, SUB, LANES)
            imag = values[rows:].reshape(GROUP, SUB, LANES)
            at = slice(line * LANES, (line + 1) * LANES)
            cos_here = cosine[:, at][None]
            sin_here = sine[:, at][None]
            steered = jnp.concatenate(
                [real * cos_here - imag * sin_here, real * sin_here + imag * cos_here], axis=1
            )
            out_ref[:, chunk * 2 * SUB : (chunk + 1) * 2 * SUB, at] = steered.astype(jnp.bfloat16)
        tail = jnp.concatenate([note, note], axis=0).astype(jnp.bfloat16)
        out_ref[:, chunk * 2 * SUB : (chunk + 1) * 2 * SUB, lines:] = jnp.broadcast_to(
            tail[None], (GROUP, 2 * SUB, LANES)
        )


def steer_part(chunks, interp, lines_total, group_hops):
    line_blocks = interp.shape[0]
    lines = line_blocks * LANES
    return pl.pallas_call(
        functools.partial(steer_kernel, lines_total, tuple(group_hops)),
        out_shape=jax.ShapeDtypeStruct((GROUP, len(chunks) * 2 * SUB, lines + LANES), jnp.bfloat16),
        scratch_shapes=[pltpu.VMEM((line_blocks + 1, GROUP * SUB, 2 * LANES), jnp.bfloat16)],
        name="steer_part",
        compiler_params=params(),
        cost_estimate=pl.CostEstimate(
            flops=STEER_COST * len(chunks), bytes_accessed=1024, transcendentals=0
        ),
    )(*chunks, interp)


def azimuth_factor(total, scale, note, hop):
    rows = note.shape[0]
    turned = note.astype(jnp.float32).T
    bins = turned[NOTE_BIN : NOTE_BIN + 1] * DIGIT + turned[NOTE_BIN + 1 : NOTE_BIN + 2]
    bins = bins.astype(jnp.int32)
    in_part = (lax.broadcasted_iota(jnp.int32, (1, rows), 1) // SUB) & 1
    groups = lax.axis_size("pulse")
    index = lax.broadcasted_iota(jnp.int32, (2 * AZ_DEV, 1), 0)
    out_part = index // AZ_DEV
    owner = lax.rem(lax.axis_index("pulse") + hop, groups)
    line = lax.axis_index("tile") * (groups * AZ_DEV) + owner * AZ_DEV + index % AZ_DEV
    turns = (line * bins + (in_part - out_part) * (total // 4)) & (total - 1)
    return (cosine_of_turns(turns, total) * scale).astype(jnp.bfloat16)


def image_kernel(total, scale, windows, first, last, *refs):
    count = len(windows)
    value_refs = refs[:count]
    if first:
        outs = refs[count:]
    else:
        before_ref, outs = refs[count], refs[count + 1 :]
    for hop in range(lax.axis_size("pulse")):
        image = None if first else before_ref[hop]
        for value_ref, pulse_rows in zip(value_refs, windows):
            rows = value_ref.shape[0] * pulse_rows
            lines = value_ref.shape[2] - LANES
            note = value_ref[:, :pulse_rows, lines:].reshape(rows, LANES)
            values = value_ref[:, :pulse_rows, :lines].reshape(rows, lines)
            factor = azimuth_factor(total, scale, note, hop)
            added = jnp.dot(factor, values, preferred_element_type=jnp.float32)
            image = added if image is None else image + added
        if not last:
            outs[0][hop] = image
        elif hop == 0:
            outs[0][...] = image
        else:
            outs[hop][...] = image.astype(jnp.bfloat16)


def image_part(values, before, last, total, scale, windows):
    groups = lax.axis_size("pulse")
    lines = values[0].shape[2] - LANES
    block = 2 * AZ_DEV
    if last:
        out_shape = (jax.ShapeDtypeStruct((block, lines), jnp.float32),) + tuple(
            jax.ShapeDtypeStruct((block, lines), jnp.bfloat16) for _ in range(groups - 1)
        )
    else:
        out_shape = jax.ShapeDtypeStruct((groups, block, lines), jnp.float32)
    operands = tuple(values) + (() if before is None else (before,))
    return pl.pallas_call(
        functools.partial(image_kernel, total, scale, tuple(windows), before is None, last),
        out_shape=out_shape,
        name="image_part",
        compiler_params=params(),
        cost_estimate=pl.CostEstimate(flops=IMAGE_COST, bytes_accessed=1024, transcendentals=0),
    )(*operands)


def local(echo, replica, interp, band_start, visible, doppler, range_step):
    half_chirp = replica.shape[1] // 2
    pulses_dev = echo.shape[1]
    lines_dev = interp.shape[0] * interp.shape[2]
    tile_count = lax.axis_size("tile")
    pulse_count = lax.axis_size("pulse")
    range_count = lax.axis_size("range")
    range_total = lines_dev * range_count
    azimuth_total = AZ_DEV * pulse_count * tile_count
    norm_scale = (pulses_dev * pulse_count * tile_count) ** (-0.5)
    far = tile_count // GROUP

    up = [(i, i + 1) for i in range(range_count - 1)]
    down = [(i + 1, i) for i in range(range_count - 1)]
    left = lax.ppermute(echo[:, :, -half_chirp:], "range", up)
    right = lax.ppermute(echo[:, :, :half_chirp], "range", down)
    *skewed, total = own_part(replica, echo)

    bands = band_start.reshape(pulses_dev, tile_count)
    mine = edge_part(left, right, skewed, total, bands, visible, range_step, doppler)

    def group_shift(hops):
        return [
            (h * GROUP + i, (h + hops) % far * GROUP + i) for h in range(far) for i in range(GROUP)
        ]

    groups = [[h * GROUP + i for i in range(GROUP)] for h in range(far)]

    def steer(chunks, group_hops):
        return steer_part(chunks, interp, range_total, group_hops)

    def exchange(steered):
        return lax.all_to_all(steered, "tile", 0, 0, axis_index_groups=groups, tiled=True)

    def add_image(values, before, last=False, windows=None):
        windows = windows or [v.shape[1] for v in values]
        return image_part(values, before, last, azimuth_total, norm_scale, windows)

    below = lax.ppermute(mine, "tile", group_shift(1))
    above = lax.ppermute(mine, "tile", group_shift(-1))
    steered = steer([mine], [far // 2])
    opposite = lax.ppermute(exchange(steered), "tile", group_shift(far // 2))
    mine, _ = lax.optimization_barrier((mine, steered))
    own = exchange(steer([mine], [0]))
    near = exchange(steer([below, above], [0, 0]))
    image = add_image([own], None)
    image = add_image([near], image)
    image = add_image([opposite], image, last=True)

    kept, *sent = image
    for hop in (2, 3, 1):
        cells = sent[hop - 1]
        pairs = [(i, (i + hop) % pulse_count) for i in range(pulse_count)]
        kept = kept + lax.ppermute(cells, "pulse", pairs).astype(jnp.float32)
    return kept.reshape(2, AZ_DEV, lines_dev)


def solution(mesh):
    in_specs = (
        P(None, ("pulse", "tile"), "range"),
        P(),
        P("range", None, None),
        P(("pulse", "tile"), None, "range"),
        P(("pulse", "tile"), None),
        P(("pulse", "tile")),
        P(("pulse", "tile")),
    )
    out_specs = P(None, ("tile", "pulse"), "range")
    return jax.shard_map(local, mesh=mesh, in_specs=in_specs, out_specs=out_specs, check_vma=False)
```

```python
import functools
import math

import jax
import jax.numpy as jnp
from jax import lax
from jax.experimental import pallas as pl
from jax.experimental.pallas import tpu as pltpu
from jax.sharding import PartitionSpec as P

AZ_DEV = 64
LANES = 128
SUB = 8
GROUP = 8
DIGIT = 128
HIDDEN = 128
NOTE_STEP = 32
NOTE_BIN = 34
VMEM_LIMIT = 14 * 1024 * 1024
IMAGE_COST = 20000000000
STEER_COST = 20000000000

SINE = tuple((-1.0) ** n * (2.0 * math.pi) ** (2 * n + 1) / math.factorial(2 * n + 1) for n in range(8))


def cosine_of_turns(turns, total):
    away = jnp.abs(turns.astype(jnp.float32) * (1.0 / total) - 0.5) - 0.25
    square = away * away
    value = jnp.full_like(away, SINE[-1])
    for factor in SINE[-2::-1]:
        value = value * square + factor
    return value * away


def params(**extra):
    return pltpu.CompilerParams(vmem_limit_bytes=VMEM_LIMIT, **extra)


def pair_rows(first, second):
    return jnp.concatenate([first, second], axis=0).astype(jnp.bfloat16)


def block_cells(ref, block):
    place = slice(block * LANES, (block + 1) * LANES)
    return jnp.concatenate(
        [ref[0, :, place].astype(jnp.float32), ref[1, :, place].astype(jnp.float32)], axis=1
    )


def arrange(ref, even_ref, odd_ref):
    blocks = ref.shape[2] // LANES
    nothing = jnp.zeros((SUB, 2 * LANES), jnp.float32)
    for pair in range(blocks // 2):
        first = block_cells(ref, 2 * pair)
        second = block_cells(ref, 2 * pair + 1)
        third = block_cells(ref, 2 * pair + 2) if 2 * pair + 2 < blocks else nothing
        even_ref[pair] = pair_rows(first, second)
        odd_ref[pair] = pair_rows(second, third)


def rows_from(even_ref, odd_ref, first, count):
    source = even_ref if first % 2 == 0 else odd_ref
    pairs = (count + 1) // 2
    start = first // 2
    return source[start : start + pairs].reshape(pairs * 2 * SUB, 2 * LANES)


def turn_matrix(real_ref, imag_ref, minus_ref, turn):
    turns = real_ref.shape[1] // LANES
    place = slice((turns - 1 - turn) * LANES, (turns - turn) * LANES)
    upper = jnp.concatenate([real_ref[:, place], minus_ref[:, place]], axis=1)
    lower = jnp.concatenate([imag_ref[:, place], real_ref[:, place]], axis=1)
    return jnp.concatenate([upper, lower], axis=0)


def own_kernel(replica_ref, own_ref, real_ref, imag_ref, minus_ref, total_ref, flip_ref, even_ref, odd_ref):
    taps = replica_ref.shape[1] // LANES
    own_blocks = own_ref.shape[2] // LANES
    half = taps // 2
    row = lax.broadcasted_iota(jnp.int32, (LANES, LANES), 0)
    column = lax.broadcasted_iota(jnp.int32, (LANES, LANES), 1)
    mirror = jnp.where(row + column == LANES - 1, 1.0, 0.0).astype(jnp.bfloat16)
    pieces = [
        replica_ref[part : part + 1, block * LANES : (block + 1) * LANES].astype(jnp.float32)
        for part in range(2)
        for block in range(taps)
    ]
    stacked = jnp.concatenate(pieces, axis=0).astype(jnp.bfloat16)
    flip_ref[...] = jnp.dot(stacked, mirror, preferred_element_type=jnp.float32)
    nothing = jnp.zeros((1, LANES), jnp.float32)
    for part, target in ((0, real_ref), (1, imag_ref)):
        base = part * taps
        for block in range(taps + 1):
            before = flip_ref[base + taps - block : base + taps - block + 1] if block else nothing
            after = flip_ref[base + taps - 1 - block : base + taps - block] if block < taps else nothing
            wide = jnp.broadcast_to(jnp.concatenate([before, after], axis=1), (LANES, 2 * LANES))
            rolled = pltpu.roll(wide, 1, 1, stride=1, stride_axis=0)[:, LANES:]
            place = slice(block * LANES, (block + 1) * LANES)
            target[:, place] = rolled.astype(jnp.bfloat16)
            if part == 1:
                minus_ref[:, place] = (-rolled).astype(jnp.bfloat16)

    arrange(own_ref, even_ref, odd_ref)
    for turn in [half] + [t for t in range(taps + 1) if t != half]:
        matrix = turn_matrix(real_ref, imag_ref, minus_ref, turn)
        first_in = max(0, turn - half)
        first_out = max(0, half - turn)
        count = own_blocks - abs(turn - half)
        window = rows_from(even_ref, odd_ref, first_in, count)
        product = jnp.dot(window, matrix, preferred_element_type=jnp.float32)
        place = slice(first_out * SUB, (first_out + count) * SUB)
        if turn == half:
            total_ref[...] = product
        else:
            total_ref[place] += product[: count * SUB]


def own_part(replica, echo):
    taps = replica.shape[1]
    blocks = echo.shape[2] // LANES
    skewed = jax.ShapeDtypeStruct((LANES, taps + LANES), jnp.bfloat16)
    cells = pltpu.VMEM((blocks // 2, 2 * SUB, 2 * LANES), jnp.bfloat16)
    return pl.pallas_call(
        own_kernel,
        out_shape=(skewed, skewed, skewed, jax.ShapeDtypeStruct((blocks * SUB, 2 * LANES), jnp.float32)),
        scratch_shapes=[pltpu.VMEM((2 * taps // LANES, LANES), jnp.float32), cells, cells],
        name="own_part",
        compiler_params=params(),
        cost_estimate=pl.CostEstimate(flops=2000000000, bytes_accessed=8 * 1024 * 1024, transcendentals=0),
    )(replica, echo)


def edge_kernel(
    step_ref, bin_ref, left_ref, right_ref, real_ref, imag_ref, minus_ref, total_ref, band_ref, visible_ref,
    out_ref, sum_ref, even_ref, odd_ref, even2_ref, odd2_ref, note_ref,
):
    rows = total_ref.shape[0]
    own_blocks = rows // SUB
    half = left_ref.shape[2] // LANES
    arrange(left_ref, even_ref, odd_ref)
    arrange(right_ref, even2_ref, odd2_ref)
    sum_ref[...] = total_ref[...]
    for turn in range(half):
        matrix = turn_matrix(real_ref, imag_ref, minus_ref, turn)
        count = half - turn
        window = rows_from(even_ref, odd_ref, turn, count)
        product = jnp.dot(window, matrix, preferred_element_type=jnp.float32)
        sum_ref[: count * SUB] += product[: count * SUB]
    for turn in range(half + 1, 2 * half + 1):
        matrix = turn_matrix(real_ref, imag_ref, minus_ref, turn)
        count = turn - half
        window = rows_from(even2_ref, odd2_ref, 0, count)
        product = jnp.dot(window, matrix, preferred_element_type=jnp.float32)
        sum_ref[(own_blocks - count) * SUB :] += product[: count * SUB]
    out_ref[:rows] = sum_ref[...].astype(jnp.bfloat16)
    pulse = lax.broadcasted_iota(jnp.int32, (SUB, LANES), 0)
    lane = lax.broadcasted_iota(jnp.int32, (SUB, LANES), 1)
    note = jnp.zeros((SUB, LANES), jnp.int32)
    for index in range(SUB):
        step = step_ref[index]
        bin_here = bin_ref[index]
        for at, digit in enumerate((step // DIGIT, step % DIGIT, bin_here // DIGIT, bin_here % DIGIT)):
            note = jnp.where((pulse == index) & (lane == NOTE_STEP + at), digit, note)
    note_ref[...] = note.astype(jnp.float32)
    bands = jnp.where(visible_ref[...] != 0, band_ref[...] // LANES, HIDDEN)
    note_ref[:, : bands.shape[1]] = bands.astype(jnp.float32)
    nothing = jnp.zeros((SUB, LANES), jnp.float32)
    out_ref[rows:, :LANES] = pair_rows(note_ref[...], nothing)
    out_ref[rows:, LANES:] = pair_rows(nothing, nothing)


def edge_part(left, right, skewed, total, bands, visible, steps, bins):
    half = left.shape[2] // LANES
    cells = pltpu.VMEM((half // 2, 2 * SUB, 2 * LANES), jnp.bfloat16)
    rows = total.shape[0]
    return pl.pallas_call(
        edge_kernel,
        out_shape=jax.ShapeDtypeStruct((rows + 2 * SUB, 2 * LANES), jnp.bfloat16),
        in_specs=[pl.BlockSpec(memory_space=pltpu.SMEM)] * 2 + [pl.BlockSpec(memory_space=pltpu.VMEM)] * 8,
        scratch_shapes=[pltpu.VMEM(total.shape, jnp.float32), cells, cells, cells, cells]
        + [pltpu.VMEM((SUB, LANES), jnp.float32)],
        name="edge_part",
        compiler_params=params(),
        cost_estimate=pl.CostEstimate(flops=300000000, bytes_accessed=4 * 1024 * 1024, transcendentals=0),
    )(steps, bins, left, right, *skewed, total, bands, visible)


def steer_kernel(lines_total, group_hops, *refs):
    chunk_refs, (interp_ref, out_ref, band_ref) = refs[:-3], refs[-3:]
    line_blocks = interp_ref.shape[0]
    lines = line_blocks * LANES
    far = lax.axis_size("tile") // GROUP
    first_line = lax.axis_index("range") * lines
    note_rows = 2 * SUB
    rows = GROUP * SUB
    for chunk, parts in enumerate(chunk_refs):
        whole = parts[...]
        count = whole.shape[0] - note_rows
        compressed = whole[:count]
        group = lax.rem(lax.axis_index("tile") // GROUP + group_hops[chunk], far)
        note = whole[count:].astype(jnp.float32)[:SUB, :LANES]
        lane = lax.broadcasted_iota(jnp.int32, (SUB, LANES), 1)

        def pick(index):
            return jnp.sum(jnp.where(lane == index, note, 0.0), axis=1, keepdims=True).astype(jnp.int32)

        pulse = lax.broadcasted_iota(jnp.int32, (SUB, 1), 0)
        wanted = jnp.concatenate([pick(group * GROUP + tile) * SUB + pulse for tile in range(GROUP)], axis=0)
        column = lax.broadcasted_iota(jnp.int32, (rows, count), 1)
        away = column - wanted
        for piece in range(line_blocks + 1):
            chooser = jnp.where(away == piece * SUB, 1.0, 0.0).astype(jnp.bfloat16)
            picked = jnp.dot(chooser, compressed, preferred_element_type=jnp.float32)
            band_ref[piece] = picked.astype(jnp.bfloat16)

        step = pick(NOTE_STEP) * DIGIT + pick(NOTE_STEP + 1)
        number = first_line + lax.broadcasted_iota(jnp.int32, (SUB, lines), 1)
        turns = (step * number) & (lines_total - 1)
        cosine = cosine_of_turns(turns, lines_total)
        sine = cosine_of_turns((turns - lines_total // 4) & (lines_total - 1), lines_total)

        for line in range(line_blocks):
            both = []
            for part in range(2):
                half = slice(part * LANES, (part + 1) * LANES)
                both.append(jnp.concatenate([band_ref[line, :, half], band_ref[line + 1, :, half]], axis=1))
            values = jnp.dot(
                jnp.concatenate(both, axis=0), interp_ref[line], preferred_element_type=jnp.float32
            )
            real = values[:rows].reshape(GROUP, SUB, LANES)
            imag = values[rows:].reshape(GROUP, SUB, LANES)
            at = slice(line * LANES, (line + 1) * LANES)
            cos_here = cosine[:, at][None]
            sin_here = sine[:, at][None]
            steered = jnp.concatenate(
                [real * cos_here - imag * sin_here, real * sin_here + imag * cos_here], axis=1
            )
            out_ref[:, chunk * 2 * SUB : (chunk + 1) * 2 * SUB, at] = steered.astype(jnp.bfloat16)
        tail = jnp.concatenate([note, note], axis=0).astype(jnp.bfloat16)
        out_ref[:, chunk * 2 * SUB : (chunk + 1) * 2 * SUB, lines:] = jnp.broadcast_to(
            tail[None], (GROUP, 2 * SUB, LANES)
        )


def steer_part(chunks, interp, lines_total, group_hops):
    line_blocks = interp.shape[0]
    lines = line_blocks * LANES
    return pl.pallas_call(
        functools.partial(steer_kernel, lines_total, tuple(group_hops)),
        out_shape=jax.ShapeDtypeStruct((GROUP, len(chunks) * 2 * SUB, lines + LANES), jnp.bfloat16),
        scratch_shapes=[pltpu.VMEM((line_blocks + 1, GROUP * SUB, 2 * LANES), jnp.bfloat16)],
        name="steer_part",
        compiler_params=params(),
        cost_estimate=pl.CostEstimate(
            flops=STEER_COST * len(chunks), bytes_accessed=1024, transcendentals=0
        ),
    )(*chunks, interp)


def azimuth_factor(total, scale, note, hop):
    rows = note.shape[0]
    turned = note.astype(jnp.float32).T
    bins = turned[NOTE_BIN : NOTE_BIN + 1] * DIGIT + turned[NOTE_BIN + 1 : NOTE_BIN + 2]
    bins = bins.astype(jnp.int32)
    in_part = (lax.broadcasted_iota(jnp.int32, (1, rows), 1) // SUB) & 1
    groups = lax.axis_size("pulse")
    index = lax.broadcasted_iota(jnp.int32, (2 * AZ_DEV, 1), 0)
    out_part = index // AZ_DEV
    owner = lax.rem(lax.axis_index("pulse") + hop, groups)
    line = lax.axis_index("tile") * (groups * AZ_DEV) + owner * AZ_DEV + index % AZ_DEV
    turns = (line * bins + (in_part - out_part) * (total // 4)) & (total - 1)
    return (cosine_of_turns(turns, total) * scale).astype(jnp.bfloat16)


def image_kernel(total, scale, windows, first, last, *refs):
    count = len(windows)
    value_refs = refs[:count]
    if first:
        outs = refs[count:]
    else:
        before_ref, outs = refs[count], refs[count + 1 :]
    for hop in range(lax.axis_size("pulse")):
        image = None if first else before_ref[hop]
        for value_ref, pulse_rows in zip(value_refs, windows):
            rows = value_ref.shape[0] * pulse_rows
            lines = value_ref.shape[2] - LANES
            note = value_ref[:, :pulse_rows, lines:].reshape(rows, LANES)
            values = value_ref[:, :pulse_rows, :lines].reshape(rows, lines)
            factor = azimuth_factor(total, scale, note, hop)
            added = jnp.dot(factor, values, preferred_element_type=jnp.float32)
            image = added if image is None else image + added
        if not last:
            outs[0][hop] = image
        elif hop == 0:
            outs[0][...] = image
        else:
            outs[hop][...] = image.astype(jnp.bfloat16)


def image_part(values, before, last, total, scale, windows):
    groups = lax.axis_size("pulse")
    lines = values[0].shape[2] - LANES
    block = 2 * AZ_DEV
    if last:
        out_shape = (jax.ShapeDtypeStruct((block, lines), jnp.float32),) + tuple(
            jax.ShapeDtypeStruct((block, lines), jnp.bfloat16) for _ in range(groups - 1)
        )
    else:
        out_shape = jax.ShapeDtypeStruct((groups, block, lines), jnp.float32)
    operands = tuple(values) + (() if before is None else (before,))
    return pl.pallas_call(
        functools.partial(image_kernel, total, scale, tuple(windows), before is None, last),
        out_shape=out_shape,
        name="image_part",
        compiler_params=params(),
        cost_estimate=pl.CostEstimate(flops=IMAGE_COST, bytes_accessed=1024, transcendentals=0),
    )(*operands)


def local(echo, replica, interp, band_start, visible, doppler, range_step):
    half_chirp = replica.shape[1] // 2
    pulses_dev = echo.shape[1]
    lines_dev = interp.shape[0] * interp.shape[2]
    tile_count = lax.axis_size("tile")
    pulse_count = lax.axis_size("pulse")
    range_count = lax.axis_size("range")
    range_total = lines_dev * range_count
    azimuth_total = AZ_DEV * pulse_count * tile_count
    norm_scale = (pulses_dev * pulse_count * tile_count) ** (-0.5)
    far = tile_count // GROUP

    up = [(i, i + 1) for i in range(range_count - 1)]
    down = [(i + 1, i) for i in range(range_count - 1)]
    left = lax.ppermute(echo[:, :, -half_chirp:], "range", up)
    right = lax.ppermute(echo[:, :, :half_chirp], "range", down)
    *skewed, total = own_part(replica, echo)

    bands = band_start.reshape(pulses_dev, tile_count)
    mine = edge_part(left, right, skewed, total, bands, visible, range_step, doppler)

    def group_shift(hops):
        return [
            (h * GROUP + i, (h + hops) % far * GROUP + i) for h in range(far) for i in range(GROUP)
        ]

    groups = [[h * GROUP + i for i in range(GROUP)] for h in range(far)]

    def steer(chunks, group_hops):
        return steer_part(chunks, interp, range_total, group_hops)

    def exchange(steered):
        return lax.all_to_all(steered, "tile", 0, 0, axis_index_groups=groups, tiled=True)

    def add_image(values, before, last=False, windows=None):
        windows = windows or [v.shape[1] for v in values]
        return image_part(values, before, last, azimuth_total, norm_scale, windows)

    below = lax.ppermute(mine, "tile", group_shift(1))
    above = lax.ppermute(mine, "tile", group_shift(-1))
    steered = steer([mine], [far // 2])
    opposite = lax.ppermute(exchange(steered), "tile", group_shift(far // 2))
    mine, _ = lax.optimization_barrier((mine, steered))
    own = exchange(steer([mine], [0]))
    near = exchange(steer([below, above], [0, 0]))
    image = add_image([own], None)
    image = add_image([near], image)
    image = add_image([opposite], image, last=True)

    kept, *sent = image
    for hop in (2, 1, 3):
        cells = sent[hop - 1]
        pairs = [(i, (i + hop) % pulse_count) for i in range(pulse_count)]
        kept = kept + lax.ppermute(cells, "pulse", pairs).astype(jnp.float32)
    return kept.reshape(2, AZ_DEV, lines_dev)


def solution(mesh):
    in_specs = (
        P(None, ("pulse", "tile"), "range"),
        P(),
        P("range", None, None),
        P(("pulse", "tile"), None, "range"),
        P(("pulse", "tile"), None),
        P(("pulse", "tile")),
        P(("pulse", "tile")),
    )
    out_specs = P(None, ("tile", "pulse"), "range")
    return jax.shard_map(local, mesh=mesh, in_specs=in_specs, out_specs=out_specs, check_vma=False)
```

```python
import functools
import math

import jax
import jax.numpy as jnp
from jax import lax
from jax.experimental import pallas as pl
from jax.experimental.pallas import tpu as pltpu
from jax.sharding import PartitionSpec as P

AZ_DEV = 64
LANES = 128
SUB = 8
GROUP = 8
DIGIT = 128
HIDDEN = 128
NOTE_STEP = 32
NOTE_BIN = 34
VMEM_LIMIT = 14 * 1024 * 1024
IMAGE_COST = 20000000000
STEER_COST = 20000000000

SINE = tuple((-1.0) ** n * (2.0 * math.pi) ** (2 * n + 1) / math.factorial(2 * n + 1) for n in range(7))


def cosine_of_turns(turns, total):
    away = jnp.abs(turns.astype(jnp.float32) * (1.0 / total) - 0.5) - 0.25
    square = away * away
    value = jnp.full_like(away, SINE[-1])
    for factor in SINE[-2::-1]:
        value = value * square + factor
    return value * away


def params(**extra):
    return pltpu.CompilerParams(vmem_limit_bytes=VMEM_LIMIT, **extra)


def pair_rows(first, second):
    return jnp.concatenate([first, second], axis=0).astype(jnp.bfloat16)


def block_cells(ref, block):
    place = slice(block * LANES, (block + 1) * LANES)
    return jnp.concatenate(
        [ref[0, :, place].astype(jnp.float32), ref[1, :, place].astype(jnp.float32)], axis=1
    )


def arrange(ref, even_ref, odd_ref):
    blocks = ref.shape[2] // LANES
    nothing = jnp.zeros((SUB, 2 * LANES), jnp.float32)
    for pair in range(blocks // 2):
        first = block_cells(ref, 2 * pair)
        second = block_cells(ref, 2 * pair + 1)
        third = block_cells(ref, 2 * pair + 2) if 2 * pair + 2 < blocks else nothing
        even_ref[pair] = pair_rows(first, second)
        odd_ref[pair] = pair_rows(second, third)


def rows_from(even_ref, odd_ref, first, count):
    source = even_ref if first % 2 == 0 else odd_ref
    pairs = (count + 1) // 2
    start = first // 2
    return source[start : start + pairs].reshape(pairs * 2 * SUB, 2 * LANES)


def turn_matrix(real_ref, imag_ref, minus_ref, turn):
    turns = real_ref.shape[1] // LANES
    place = slice((turns - 1 - turn) * LANES, (turns - turn) * LANES)
    upper = jnp.concatenate([real_ref[:, place], minus_ref[:, place]], axis=1)
    lower = jnp.concatenate([imag_ref[:, place], real_ref[:, place]], axis=1)
    return jnp.concatenate([upper, lower], axis=0)


def own_kernel(replica_ref, own_ref, real_ref, imag_ref, minus_ref, total_ref, flip_ref, even_ref, odd_ref):
    taps = replica_ref.shape[1] // LANES
    own_blocks = own_ref.shape[2] // LANES
    half = taps // 2
    row = lax.broadcasted_iota(jnp.int32, (LANES, LANES), 0)
    column = lax.broadcasted_iota(jnp.int32, (LANES, LANES), 1)
    mirror = jnp.where(row + column == LANES - 1, 1.0, 0.0).astype(jnp.bfloat16)
    pieces = [
        replica_ref[part : part + 1, block * LANES : (block + 1) * LANES].astype(jnp.float32)
        for part in range(2)
        for block in range(taps)
    ]
    stacked = jnp.concatenate(pieces, axis=0).astype(jnp.bfloat16)
    flip_ref[...] = jnp.dot(stacked, mirror, preferred_element_type=jnp.float32)
    nothing = jnp.zeros((1, LANES), jnp.float32)
    for part, target in ((0, real_ref), (1, imag_ref)):
        base = part * taps
        for block in range(taps + 1):
            before = flip_ref[base + taps - block : base + taps - block + 1] if block else nothing
            after = flip_ref[base + taps - 1 - block : base + taps - block] if block < taps else nothing
            wide = jnp.broadcast_to(jnp.concatenate([before, after], axis=1), (LANES, 2 * LANES))
            rolled = pltpu.roll(wide, 1, 1, stride=1, stride_axis=0)[:, LANES:]
            place = slice(block * LANES, (block + 1) * LANES)
            target[:, place] = rolled.astype(jnp.bfloat16)
            if part == 1:
                minus_ref[:, place] = (-rolled).astype(jnp.bfloat16)

    arrange(own_ref, even_ref, odd_ref)
    for turn in [half] + [t for t in range(taps + 1) if t != half]:
        matrix = turn_matrix(real_ref, imag_ref, minus_ref, turn)
        first_in = max(0, turn - half)
        first_out = max(0, half - turn)
        count = own_blocks - abs(turn - half)
        window = rows_from(even_ref, odd_ref, first_in, count)
        product = jnp.dot(window, matrix, preferred_element_type=jnp.float32)
        place = slice(first_out * SUB, (first_out + count) * SUB)
        if turn == half:
            total_ref[...] = product
        else:
            total_ref[place] += product[: count * SUB]


def own_part(replica, echo):
    taps = replica.shape[1]
    blocks = echo.shape[2] // LANES
    skewed = jax.ShapeDtypeStruct((LANES, taps + LANES), jnp.bfloat16)
    cells = pltpu.VMEM((blocks // 2, 2 * SUB, 2 * LANES), jnp.bfloat16)
    return pl.pallas_call(
        own_kernel,
        out_shape=(skewed, skewed, skewed, jax.ShapeDtypeStruct((blocks * SUB, 2 * LANES), jnp.float32)),
        scratch_shapes=[pltpu.VMEM((2 * taps // LANES, LANES), jnp.float32), cells, cells],
        name="own_part",
        compiler_params=params(),
        cost_estimate=pl.CostEstimate(flops=2000000000, bytes_accessed=8 * 1024 * 1024, transcendentals=0),
    )(replica, echo)


def edge_kernel(
    step_ref, bin_ref, left_ref, right_ref, real_ref, imag_ref, minus_ref, total_ref, band_ref, visible_ref,
    out_ref, sum_ref, even_ref, odd_ref, even2_ref, odd2_ref, note_ref,
):
    rows = total_ref.shape[0]
    own_blocks = rows // SUB
    half = left_ref.shape[2] // LANES
    arrange(left_ref, even_ref, odd_ref)
    arrange(right_ref, even2_ref, odd2_ref)
    sum_ref[...] = total_ref[...]
    for turn in range(half):
        matrix = turn_matrix(real_ref, imag_ref, minus_ref, turn)
        count = half - turn
        window = rows_from(even_ref, odd_ref, turn, count)
        product = jnp.dot(window, matrix, preferred_element_type=jnp.float32)
        sum_ref[: count * SUB] += product[: count * SUB]
    for turn in range(half + 1, 2 * half + 1):
        matrix = turn_matrix(real_ref, imag_ref, minus_ref, turn)
        count = turn - half
        window = rows_from(even2_ref, odd2_ref, 0, count)
        product = jnp.dot(window, matrix, preferred_element_type=jnp.float32)
        sum_ref[(own_blocks - count) * SUB :] += product[: count * SUB]
    out_ref[:rows] = sum_ref[...].astype(jnp.bfloat16)
    pulse = lax.broadcasted_iota(jnp.int32, (SUB, LANES), 0)
    lane = lax.broadcasted_iota(jnp.int32, (SUB, LANES), 1)
    note = jnp.zeros((SUB, LANES), jnp.int32)
    for index in range(SUB):
        step = step_ref[index]
        bin_here = bin_ref[index]
        for at, digit in enumerate((step // DIGIT, step % DIGIT, bin_here // DIGIT, bin_here % DIGIT)):
            note = jnp.where((pulse == index) & (lane == NOTE_STEP + at), digit, note)
    note_ref[...] = note.astype(jnp.float32)
    bands = jnp.where(visible_ref[...] != 0, band_ref[...] // LANES, HIDDEN)
    note_ref[:, : bands.shape[1]] = bands.astype(jnp.float32)
    nothing = jnp.zeros((SUB, LANES), jnp.float32)
    out_ref[rows:, :LANES] = pair_rows(note_ref[...], nothing)
    out_ref[rows:, LANES:] = pair_rows(nothing, nothing)


def edge_part(left, right, skewed, total, bands, visible, steps, bins):
    half = left.shape[2] // LANES
    cells = pltpu.VMEM((half // 2, 2 * SUB, 2 * LANES), jnp.bfloat16)
    rows = total.shape[0]
    return pl.pallas_call(
        edge_kernel,
        out_shape=jax.ShapeDtypeStruct((rows + 2 * SUB, 2 * LANES), jnp.bfloat16),
        in_specs=[pl.BlockSpec(memory_space=pltpu.SMEM)] * 2 + [pl.BlockSpec(memory_space=pltpu.VMEM)] * 8,
        scratch_shapes=[pltpu.VMEM(total.shape, jnp.float32), cells, cells, cells, cells]
        + [pltpu.VMEM((SUB, LANES), jnp.float32)],
        name="edge_part",
        compiler_params=params(),
        cost_estimate=pl.CostEstimate(flops=300000000, bytes_accessed=4 * 1024 * 1024, transcendentals=0),
    )(steps, bins, left, right, *skewed, total, bands, visible)


def steer_kernel(lines_total, group_hops, *refs):
    chunk_refs, (interp_ref, out_ref, band_ref) = refs[:-3], refs[-3:]
    line_blocks = interp_ref.shape[0]
    lines = line_blocks * LANES
    far = lax.axis_size("tile") // GROUP
    first_line = lax.axis_index("range") * lines
    note_rows = 2 * SUB
    rows = GROUP * SUB
    for chunk, parts in enumerate(chunk_refs):
        whole = parts[...]
        count = whole.shape[0] - note_rows
        compressed = whole[:count]
        group = lax.rem(lax.axis_index("tile") // GROUP + group_hops[chunk], far)
        note = whole[count:].astype(jnp.float32)[:SUB, :LANES]
        lane = lax.broadcasted_iota(jnp.int32, (SUB, LANES), 1)

        def pick(index):
            return jnp.sum(jnp.where(lane == index, note, 0.0), axis=1, keepdims=True).astype(jnp.int32)

        pulse = lax.broadcasted_iota(jnp.int32, (SUB, 1), 0)
        wanted = jnp.concatenate([pick(group * GROUP + tile) * SUB + pulse for tile in range(GROUP)], axis=0)
        column = lax.broadcasted_iota(jnp.int32, (rows, count), 1)
        away = column - wanted
        for piece in range(line_blocks + 1):
            chooser = jnp.where(away == piece * SUB, 1.0, 0.0).astype(jnp.bfloat16)
            picked = jnp.dot(chooser, compressed, preferred_element_type=jnp.float32)
            band_ref[piece] = picked.astype(jnp.bfloat16)

        step = pick(NOTE_STEP) * DIGIT + pick(NOTE_STEP + 1)
        number = first_line + lax.broadcasted_iota(jnp.int32, (SUB, lines), 1)
        turns = (step * number) & (lines_total - 1)
        cosine = cosine_of_turns(turns, lines_total)
        sine = cosine_of_turns((turns - lines_total // 4) & (lines_total - 1), lines_total)

        for line in range(line_blocks):
            both = []
            for part in range(2):
                half = slice(part * LANES, (part + 1) * LANES)
                both.append(jnp.concatenate([band_ref[line, :, half], band_ref[line + 1, :, half]], axis=1))
            values = jnp.dot(
                jnp.concatenate(both, axis=0), interp_ref[line], preferred_element_type=jnp.float32
            )
            real = values[:rows].reshape(GROUP, SUB, LANES)
            imag = values[rows:].reshape(GROUP, SUB, LANES)
            at = slice(line * LANES, (line + 1) * LANES)
            cos_here = cosine[:, at][None]
            sin_here = sine[:, at][None]
            steered = jnp.concatenate(
                [real * cos_here - imag * sin_here, real * sin_here + imag * cos_here], axis=1
            )
            out_ref[:, chunk * 2 * SUB : (chunk + 1) * 2 * SUB, at] = steered.astype(jnp.bfloat16)
        tail = jnp.concatenate([note, note], axis=0).astype(jnp.bfloat16)
        out_ref[:, chunk * 2 * SUB : (chunk + 1) * 2 * SUB, lines:] = jnp.broadcast_to(
            tail[None], (GROUP, 2 * SUB, LANES)
        )


def steer_part(chunks, interp, lines_total, group_hops):
    line_blocks = interp.shape[0]
    lines = line_blocks * LANES
    return pl.pallas_call(
        functools.partial(steer_kernel, lines_total, tuple(group_hops)),
        out_shape=jax.ShapeDtypeStruct((GROUP, len(chunks) * 2 * SUB, lines + LANES), jnp.bfloat16),
        scratch_shapes=[pltpu.VMEM((line_blocks + 1, GROUP * SUB, 2 * LANES), jnp.bfloat16)],
        name="steer_part",
        compiler_params=params(),
        cost_estimate=pl.CostEstimate(
            flops=STEER_COST * len(chunks), bytes_accessed=1024, transcendentals=0
        ),
    )(*chunks, interp)


def azimuth_factor(total, scale, note, hop):
    rows = note.shape[0]
    turned = note.astype(jnp.float32).T
    bins = turned[NOTE_BIN : NOTE_BIN + 1] * DIGIT + turned[NOTE_BIN + 1 : NOTE_BIN + 2]
    bins = bins.astype(jnp.int32)
    in_part = (lax.broadcasted_iota(jnp.int32, (1, rows), 1) // SUB) & 1
    groups = lax.axis_size("pulse")
    index = lax.broadcasted_iota(jnp.int32, (2 * AZ_DEV, 1), 0)
    out_part = index // AZ_DEV
    owner = lax.rem(lax.axis_index("pulse") + hop, groups)
    line = lax.axis_index("tile") * (groups * AZ_DEV) + owner * AZ_DEV + index % AZ_DEV
    turns = (line * bins + (in_part - out_part) * (total // 4)) & (total - 1)
    return (cosine_of_turns(turns, total) * scale).astype(jnp.bfloat16)


def image_kernel(total, scale, windows, first, last, *refs):
    count = len(windows)
    value_refs = refs[:count]
    if first:
        outs = refs[count:]
    else:
        before_ref, outs = refs[count], refs[count + 1 :]
    for hop in range(lax.axis_size("pulse")):
        image = None if first else before_ref[hop]
        for value_ref, pulse_rows in zip(value_refs, windows):
            rows = value_ref.shape[0] * pulse_rows
            lines = value_ref.shape[2] - LANES
            note = value_ref[:, :pulse_rows, lines:].reshape(rows, LANES)
            values = value_ref[:, :pulse_rows, :lines].reshape(rows, lines)
            factor = azimuth_factor(total, scale, note, hop)
            added = jnp.dot(factor, values, preferred_element_type=jnp.float32)
            image = added if image is None else image + added
        if not last:
            outs[0][hop] = image
        elif hop == 0:
            outs[0][...] = image
        else:
            outs[hop][...] = image.astype(jnp.bfloat16)


def image_part(values, before, last, total, scale, windows):
    groups = lax.axis_size("pulse")
    lines = values[0].shape[2] - LANES
    block = 2 * AZ_DEV
    if last:
        out_shape = (jax.ShapeDtypeStruct((block, lines), jnp.float32),) + tuple(
            jax.ShapeDtypeStruct((block, lines), jnp.bfloat16) for _ in range(groups - 1)
        )
    else:
        out_shape = jax.ShapeDtypeStruct((groups, block, lines), jnp.float32)
    operands = tuple(values) + (() if before is None else (before,))
    return pl.pallas_call(
        functools.partial(image_kernel, total, scale, tuple(windows), before is None, last),
        out_shape=out_shape,
        name="image_part",
        compiler_params=params(),
        cost_estimate=pl.CostEstimate(flops=IMAGE_COST, bytes_accessed=1024, transcendentals=0),
    )(*operands)


def local(echo, replica, interp, band_start, visible, doppler, range_step):
    half_chirp = replica.shape[1] // 2
    pulses_dev = echo.shape[1]
    lines_dev = interp.shape[0] * interp.shape[2]
    tile_count = lax.axis_size("tile")
    pulse_count = lax.axis_size("pulse")
    range_count = lax.axis_size("range")
    range_total = lines_dev * range_count
    azimuth_total = AZ_DEV * pulse_count * tile_count
    norm_scale = (pulses_dev * pulse_count * tile_count) ** (-0.5)
    far = tile_count // GROUP

    up = [(i, i + 1) for i in range(range_count - 1)]
    down = [(i + 1, i) for i in range(range_count - 1)]
    left = lax.ppermute(echo[:, :, -half_chirp:], "range", up)
    right = lax.ppermute(echo[:, :, :half_chirp], "range", down)
    *skewed, total = own_part(replica, echo)

    bands = band_start.reshape(pulses_dev, tile_count)
    mine = edge_part(left, right, skewed, total, bands, visible, range_step, doppler)

    def group_shift(hops):
        return [
            (h * GROUP + i, (h + hops) % far * GROUP + i) for h in range(far) for i in range(GROUP)
        ]

    groups = [[h * GROUP + i for i in range(GROUP)] for h in range(far)]

    def steer(chunks, group_hops):
        return steer_part(chunks, interp, range_total, group_hops)

    def exchange(steered):
        return lax.all_to_all(steered, "tile", 0, 0, axis_index_groups=groups, tiled=True)

    def add_image(values, before, last=False, windows=None):
        windows = windows or [v.shape[1] for v in values]
        return image_part(values, before, last, azimuth_total, norm_scale, windows)

    below = lax.ppermute(mine, "tile", group_shift(1))
    above = lax.ppermute(mine, "tile", group_shift(-1))
    steered = steer([mine], [far // 2])
    opposite = lax.ppermute(exchange(steered), "tile", group_shift(far // 2))
    mine, _ = lax.optimization_barrier((mine, steered))
    own = exchange(steer([mine], [0]))
    near = exchange(steer([below, above], [0, 0]))
    image = add_image([own], None)
    image = add_image([near], image)
    image = add_image([opposite], image, last=True)

    kept, *sent = image
    for hop in (2, 3, 1):
        cells = sent[hop - 1]
        pairs = [(i, (i + hop) % pulse_count) for i in range(pulse_count)]
        kept = kept + lax.ppermute(cells, "pulse", pairs).astype(jnp.float32)
    return kept.reshape(2, AZ_DEV, lines_dev)


def solution(mesh):
    in_specs = (
        P(None, ("pulse", "tile"), "range"),
        P(),
        P("range", None, None),
        P(("pulse", "tile"), None, "range"),
        P(("pulse", "tile"), None),
        P(("pulse", "tile")),
        P(("pulse", "tile")),
    )
    out_specs = P(None, ("tile", "pulse"), "range")
    return jax.shard_map(local, mesh=mesh, in_specs=in_specs, out_specs=out_specs, check_vma=False)
```
